256 devices in a mesh: req: 4 (over x), exp: 64 (over z, y, core).
Axes of the slice: x: 4, y: 4, z: 8, core: 2. Of those that a mesh axis runs over, the one named last changes fastest.
Arguments:
- hidden: bfloat16 [256, 32, 2048], P(('req', 'exp')), may hold values from -6 to 6
- queries: bfloat16 [256, 32, 3072], P(('req', 'exp'))
- new_latent: bfloat16 [256, 32, 576], P(('req', 'exp')), may hold values from -6 to 6
- pages: bfloat16 [2048, 128, 576], P(('req', 'exp'))
- page_table: int32 [256, 8], P(('req', 'exp')), may hold values from 0 to 7, each once within a row
- cache_len: int32 [256], P(('req', 'exp')), may hold values from 1 to 992, as said below
- parents: int32 [256, 32], P(('req', 'exp')), may hold values from 0 to 30, as said below
- accept_path: int32 [256, 32], P(('req', 'exp')), may hold values from 0 to 31, as said below
- accept_count: int32 [256], P(('req', 'exp')), may hold values from 1 to 32, as said below
- key_up: bfloat16 [16, 128, 512], replicated, may hold values from -0.5 to 0.5
- value_up: bfloat16 [16, 512, 128], replicated, may hold values from -0.25 to 0.25
- out_proj: bfloat16 [2048, 2048], P(None, 'req'), may hold values from -0.125 to 0.125
- norm_gain: bfloat16 [2048], replicated, may hold values from 0.5 to 1.5
- route_ids: int32 [4, 64, 32, 6], P(None, 'exp'), may hold values from 0 to 63, all different within a row; in each aligned block of 32 rows (0 to 31, 32 to 63, ..., all dimensions but the last counted through in order) at most 6 rows name the same one
- route_weights: float32 [4, 64, 32, 6], P(None, 'exp'), may hold values from 0.2 to 1.2
- w_gate: bfloat16 [64, 2048, 1408], P('exp', None, 'req'), may hold values from -0.125 to 0.125
- w_up: bfloat16 [64, 2048, 1408], P('exp', None, 'req'), may hold values from -0.125 to 0.125
- w_down: bfloat16 [64, 1408, 2048], P('exp', 'req'), may hold values from -0.15625 to 0.15625
Outputs:
- layer_out: bfloat16 [256, 32, 2048], P(('req', 'exp'))
- new_pages: bfloat16 [2048, 128, 576], P(('req', 'exp'))
The draws below stay inside these ranges and needn't reach their ends.
Inputs may be any that keep to these rules, and one draw needn't show every extreme that they name: `route_ids`: in each request no expert is named by more than 6 tokens, a bound that some block reaches. `page_table`: each row is an order of the 8 pages of the request's pool. `cache_len`: some request holds the largest length. parents[q, 0] = 0; for t >= 1 the parent of t is below t; one request's tree is a single chain. `accept_path`: entry k for k < accept_count is the ancestor at depth k of the last accepted token, entry 0 the root; later entries are 0. `accept_count`: one more than the depth of the last accepted token.
All inputs are finite; a program needn't handle non-finite values.
Results may differ from the reference program's by a relative error of at most 0.023.
Values may be sent and summed in bfloat16 or wider, within the bound.
A program may use at most 128 MiB of HBM per device.

```python
import math
import jax
import jax.numpy as jnp
import numpy as np
from jax import lax

D = 2048
HEADS = 16
NOPE = 128
ROPE = 64
LAT = 512
VDIM = 128
FF = 1408
TOP = 6
TREE = 32
PAGE = 128
PAGES_DEV = 8
EXPERTS = 64
REQS = 256
CAP = 6
N_REQ = 4
N_EXP = 64


def draw_queries(key, part):
    base = jax.random.normal(jax.random.fold_in(key, 1), (REQS, TREE, HEADS, NOPE + ROPE), jnp.float32)
    base = jnp.clip(base, -6.0, 6.0)
    return base.reshape(REQS, TREE, HEADS * (NOPE + ROPE)).astype(jnp.bfloat16)


def draw_pages(key, part):
    base = jax.random.normal(jax.random.fold_in(key, 3), (REQS * PAGES_DEV, PAGE, LAT + ROPE), jnp.float32)
    base = jnp.clip(base, -6.0, 6.0)
    return base.astype(jnp.bfloat16)


def draw_cache_len(key, part):
    longest = PAGES_DEV * PAGE - TREE
    lengths = 1 + jax.random.randint(jax.random.fold_in(key, 5), (REQS,), 0, longest)
    holder = jax.random.randint(jax.random.fold_in(key, 6), (), 0, REQS)
    lengths = jnp.where(jnp.arange(REQS) == holder, longest, lengths)
    return lengths.astype(jnp.int32)


def tree_parts(key):
    base_key = jax.random.fold_in(key, 4242)
    raw = jax.random.randint(jax.random.fold_in(base_key, 1), (REQS, TREE), 0, 1 << 20)
    token_ids = jnp.arange(TREE, dtype=jnp.int32)
    request_ids = jnp.arange(REQS, dtype=jnp.int32)
    chain_req = jax.random.randint(jax.random.fold_in(base_key, 3), (), 0, REQS)
    parent_ids = raw % jnp.maximum(token_ids, 1)[None, :]
    chain_parent = jnp.maximum(token_ids - 1, 0)[None, :]
    parent_ids = jnp.where(request_ids[:, None] == chain_req, chain_parent, parent_ids)
    parent_ids = jnp.where(token_ids[None, :] == 0, 0, parent_ids)
    parent_ids = jnp.where(token_ids[None, :] == TREE - 1, TREE - 2, parent_ids).astype(jnp.int32)
    depth = jnp.zeros((REQS, TREE), jnp.int32)
    for index in range(1, TREE):
        above = jnp.take_along_axis(depth, parent_ids[:, index:index + 1], axis=1)[:, 0]
        depth = depth.at[:, index].set(above + 1)
    chosen = jax.random.randint(jax.random.fold_in(base_key, 2), (REQS,), 0, TREE).astype(jnp.int32)
    chosen = jnp.where(request_ids == chain_req, TREE - 1, chosen).astype(jnp.int32)
    chosen_depth = jnp.take_along_axis(depth, chosen[:, None], axis=1)[:, 0]
    path = jnp.zeros((REQS, TREE), jnp.int32)
    current = chosen
    for index in range(TREE):
        level = jnp.take_along_axis(depth, current[:, None], axis=1)[:, 0]
        path = jnp.where(token_ids[None, :] == level[:, None], current[:, None], path)
        current = jnp.take_along_axis(parent_ids, current[:, None], axis=1)[:, 0]
    return (parent_ids, path.astype(jnp.int32), (chosen_depth + 1).astype(jnp.int32))


def draw_parents(key, part):
    return tree_parts(key)[0]


def draw_accept_path(key, part):
    return tree_parts(key)[1]


def draw_accept_count(key, part):
    return tree_parts(key)[2]


def steps_of(stream_key, shape, shards, smallest, high):
    def one(axis_at, parts):
        heights = jax.random.uniform(jax.random.fold_in(jax.random.fold_in(stream_key, 6), axis_at), (parts,), jnp.float32, smallest / len(shards), high / len(shards))
        return jnp.repeat(jnp.exp(heights), shape[axis_at] // parts).reshape((-1,) + (1,) * (len(shape) - axis_at - 1))

    level = one(*shards[0])
    for cut in shards[1:]:
        level = level * one(*cut)
    return level


def deal_out(stream_key, own, number, rows, count, top, most, lean):
    sequence = jax.random.permutation(stream_key, count)
    packed, ordinary = shares(count, rows * top, most, lean, True), shares(count, rows * top, most, lean, False)
    places = jnp.arange(count)

    def named(tallies, offset_by):
        used = int((tallies > 0).sum())
        fixed = max(1, used // 4)
        moved = fixed + (places - fixed + offset_by * (used - fixed)) % max(1, count - fixed)
        return jnp.zeros((count,), jnp.int32).at[sequence[jnp.where(places < fixed, places, moved)]].set(jnp.asarray(tallies, jnp.int32))

    tallies = jnp.where(number % 4 == 0, named(packed, number // 4), named(ordinary, number - number // 4 - 1))
    mixed = jax.random.permutation(jax.random.fold_in(own, 3), count)
    source_of, sink = mixed[0:count // 2 * 2:2], mixed[1:count // 2 * 2:2]
    slack = jnp.minimum(tallies[source_of] - 1, most - tallies[sink]) // 2
    slack = jnp.where((source_of == sequence[0]) | (sink == sequence[0]) | (tallies[sink] == 0), 0, jnp.maximum(slack, 0))
    moved = jax.random.randint(jax.random.fold_in(own, 4), (count // 2,), 0, 1 << 20) % (slack + 1)
    tallies = tallies.at[source_of].add(-moved).at[sink].add(moved)
    members = jnp.searchsorted(jnp.cumsum(tallies), jnp.arange(rows * top), side="right").astype(jnp.int32)
    listing = members.reshape(top, rows).T
    listing = listing[jax.random.permutation(jax.random.fold_in(own, 1), rows)]
    offset_by = jax.random.randint(jax.random.fold_in(own, 2), (rows, 1), 0, top)
    return jnp.take_along_axis(listing, (jnp.arange(top)[None, :] + offset_by) % top, axis=1)


def shares(number_of, total, most, lean, full):
    loads = [(1 << 20) // math.isqrt(standing ** lean) + 1 for standing in range(1, number_of + 1)]
    largest = most if full else min(most, max(-(-total // number_of), total * loads[0] // sum(loads)))
    least = 1 if total - largest >= number_of - 1 else 0
    counts, rest = [largest] + [least] * (number_of - 1), total - largest - least * (number_of - 1)
    while rest > 0:
        candidates = [i for i in range(1, number_of) if counts[i] < largest] or [i for i in range(1, number_of) if counts[i] < most]
        pool, left = sum([loads[i] for i in candidates]), rest
        for i in candidates:
            more = min(most - counts[i], max(1, left * loads[i] // pool), rest)
            counts[i] = counts[i] + more
            rest = rest - more
    return np.array(counts)


def normal_values(own_key, dims, deviation, bound, split=(), kind=jnp.bfloat16):
    factor_of = steps_of(own_key, dims, split, -0.22, 0.18) if split else 1.0
    entries = jax.random.normal(own_key, dims, jnp.float32) * deviation * factor_of
    return jnp.minimum(jnp.maximum(entries, -bound), bound).astype(kind)


def setup_inputs(seed: int = 0) -> dict:
    keys = jax.random.split(jax.random.key(seed), 19)
    hidden = normal_values(keys[0], (REQS, TREE, D), 1.0, 6.0, ((0, 256),))
    queries = draw_queries(jax.random.fold_in(keys[18], 71), 0)
    new_latent = normal_values(keys[2], (REQS, TREE, LAT + ROPE), 1.0, 6.0, ((0, 256),))
    pages = draw_pages(jax.random.fold_in(keys[18], 71), 0)
    page_table = jax.vmap(lambda own: jax.random.permutation(own, PAGES_DEV))(jax.random.split(keys[4], REQS)).reshape((REQS, PAGES_DEV)).astype(jnp.int32)
    cache_len = draw_cache_len(jax.random.fold_in(keys[18], 71), 0)
    parents = draw_parents(jax.random.fold_in(keys[18], 71), 0)
    accept_path = draw_accept_path(jax.random.fold_in(keys[18], 71), 0)
    accept_count = draw_accept_count(jax.random.fold_in(keys[18], 71), 0)
    key_up = normal_values(keys[9], (HEADS, NOPE, LAT), NOPE ** -0.5, 0.5)
    value_up = normal_values(keys[10], (HEADS, LAT, VDIM), LAT ** -0.5, 0.25)
    out_proj = normal_values(keys[11], (HEADS * VDIM, D), (HEADS * VDIM) ** -0.5, 0.125, ((1, 4),))
    norm_gain = jnp.clip(1.0 + 0.1 * jax.random.normal(keys[12], (D,), jnp.float32), 0.5, 1.5).astype(jnp.bfloat16)
    route_ids_keys = jax.random.split(jax.random.fold_in(keys[13], 1), N_REQ * N_EXP * TREE // TREE)
    route_ids_turns = jax.random.permutation(jax.random.fold_in(keys[13], 3), N_REQ * N_EXP * TREE // TREE)
    route_ids = jax.vmap(lambda own, number: deal_out(jax.random.fold_in(keys[13], 2), own, number, TREE, EXPERTS, TOP, CAP, 2))(route_ids_keys, route_ids_turns).reshape((N_REQ, N_EXP, TREE, TOP))
    route_weights = jnp.clip(0.2 + 1 * jax.random.uniform(keys[14], (N_REQ, N_EXP, TREE, TOP), jnp.float32) ** steps_of(keys[14], (N_REQ, N_EXP, TREE, TOP), ((1, 64),), -0.2, 0.2), 0.2, 1.2)
    w_gate = normal_values(keys[15], (EXPERTS, D, FF), D ** -0.5, 0.125, ((0, 64), (2, 4)))
    w_up = normal_values(keys[16], (EXPERTS, D, FF), D ** -0.5, 0.125, ((0, 64), (2, 4)))
    w_down = normal_values(keys[17], (EXPERTS, FF, D), FF ** -0.5, 0.15625, ((0, 64), (1, 4)))
    return {"hidden": hidden, "queries": queries, "new_latent": new_latent, "pages": pages, "page_table": page_table, "cache_len": cache_len, "parents": parents, "accept_path": accept_path, "accept_count": accept_count, "key_up": key_up, "value_up": value_up, "out_proj": out_proj, "norm_gain": norm_gain, "route_ids": route_ids, "route_weights": route_weights, "w_gate": w_gate, "w_up": w_up, "w_down": w_down}


def ancestry(parent_row):
    count = parent_row.shape[0]
    ident = jnp.eye(count, dtype=jnp.int32)
    linked = (parent_row[:, None] == jnp.arange(count, dtype=jnp.int32)[None, :]).astype(jnp.int32)
    reach = jnp.minimum(ident + linked, 1)
    for sweep in range(count.bit_length()):
        reach = jnp.minimum(jnp.dot(reach, reach), 1)
    return reach

def attend(query_row, page_pool, table_row, length, parent_row, fresh, key_up, value_up):
    count = query_row.shape[0]
    heads = key_up.shape[0]
    nope = key_up.shape[1]
    latent = key_up.shape[2]
    shaped = query_row.reshape(count, heads, -1)
    scale = 1.0 / math.sqrt(shaped.shape[2])
    q_nope = shaped[:, :, :nope]
    q_rope = shaped[:, :, nope:]
    q_latent = jnp.einsum('thn,hnc->thc', q_nope.astype(jnp.float32), key_up.astype(jnp.float32)).astype(jnp.bfloat16)
    q_full = jnp.concatenate([q_latent, q_rope], axis=2).astype(jnp.float32)
    cache_rows = jnp.take(page_pool, table_row, axis=0).reshape(-1, page_pool.shape[2])
    score_cache = jnp.einsum('thc,kc->thk', q_full, cache_rows.astype(jnp.float32)) * scale
    score_tree = jnp.einsum('thc,jc->thj', q_full, fresh.astype(jnp.float32)) * scale
    live = jnp.arange(cache_rows.shape[0], dtype=jnp.int32) < length
    score_cache = jnp.where(live[None, None, :], score_cache, -1e+30)
    score_tree = jnp.where(ancestry(parent_row)[:, None, :] > 0, score_tree, -1e+30)
    peak = jnp.maximum(lax.optimization_barrier(jnp.max(score_cache, axis=2)), lax.optimization_barrier(jnp.max(score_tree, axis=2)))[:, :, None]
    exp_cache = jnp.exp(score_cache - peak)
    exp_tree = jnp.exp(score_tree - peak)
    total = lax.optimization_barrier(jnp.sum(exp_cache, axis=2, keepdims=True)) + lax.optimization_barrier(jnp.sum(exp_tree, axis=2, keepdims=True))
    prob_cache = (exp_cache / total).astype(jnp.bfloat16)
    prob_tree = (exp_tree / total).astype(jnp.bfloat16)
    context = jnp.einsum('thk,kc->thc', prob_cache.astype(jnp.float32), cache_rows[:, :latent].astype(jnp.float32))
    context = context + jnp.einsum('thj,jc->thc', prob_tree.astype(jnp.float32), fresh[:, :latent].astype(jnp.float32))
    context = context.astype(jnp.bfloat16)
    head_out = jnp.einsum('thc,hcv->thv', context.astype(jnp.float32), value_up.astype(jnp.float32)).astype(jnp.bfloat16)
    return head_out.reshape(count, -1)

def write_rows(page_pool, table_row, length, path_row, count, fresh):
    pool_len = page_pool.shape[0]
    page_size = page_pool.shape[1]
    pool_ids = jnp.arange(pool_len, dtype=jnp.int32)
    match = table_row[None, :] == pool_ids[:, None]
    logical = lax.optimization_barrier(jnp.sum(jnp.where(match, pool_ids[None, :], 0), axis=1)).astype(jnp.int32)
    position = logical[:, None] * page_size + jnp.arange(page_size, dtype=jnp.int32)[None, :]
    offset = position - length
    valid = (offset >= 0) & (offset < count)
    source = jnp.take(path_row, jnp.clip(offset, 0, path_row.shape[0] - 1))
    written = jnp.take(fresh, source, axis=0)
    return jnp.where(valid[:, :, None], written, page_pool)

def reference(hidden, queries, new_latent, pages, page_table, cache_len, parents, accept_path, accept_count, key_up, value_up, out_proj, norm_gain, route_ids, route_weights, w_gate, w_up, w_down):
    pools = pages.reshape(REQS, PAGES_DEV, PAGE, LAT + ROPE)

    def one_request(index):
        return attend(queries[index], pools[index], page_table[index], cache_len[index], parents[index], new_latent[index], key_up, value_up)
    heads_all = lax.map(one_request, jnp.arange(REQS, dtype=jnp.int32))
    projected = jnp.dot(heads_all.reshape(-1, HEADS * VDIM), out_proj, preferred_element_type=jnp.float32).astype(jnp.bfloat16)
    mixed = (hidden.reshape(-1, D).astype(jnp.float32) + projected.astype(jnp.float32)).astype(jnp.bfloat16)
    mixed_f = mixed.astype(jnp.float32)
    normed = (mixed_f * lax.rsqrt(lax.optimization_barrier(jnp.mean(mixed_f * mixed_f, axis=1, keepdims=True)) + 1e-06) * norm_gain.astype(jnp.float32)).astype(jnp.bfloat16)
    id_rows = route_ids.reshape(REQS, TREE, TOP)
    weight_rows = route_weights.reshape(REQS, TREE, TOP)
    expert_ids = jnp.arange(EXPERTS, dtype=jnp.int32)
    hits = id_rows[:, :, :, None] == expert_ids
    chosen = lax.optimization_barrier(jnp.sum(hits.astype(jnp.int32), axis=2))
    weight_by = lax.optimization_barrier(jnp.sum(jnp.where(hits, weight_rows[:, :, :, None], 0.0), axis=2))
    before = jnp.cumsum(chosen, axis=1) - chosen
    normed3 = normed.reshape(REQS, TREE, D).astype(jnp.float32)
    slot_ids = jnp.arange(CAP, dtype=jnp.int32)
    quarter = FF // N_REQ

    def per_expert(accum, expert):
        taken = lax.dynamic_index_in_dim(chosen, expert, 2, keepdims=False)
        order = lax.dynamic_index_in_dim(before, expert, 2, keepdims=False)
        weight_col = lax.dynamic_index_in_dim(weight_by, expert, 2, keepdims=False)
        placed = ((taken > 0)[:, None, :] & (order[:, None, :] == slot_ids[None, :, None])).astype(jnp.float32)
        slot_block = jnp.einsum('qct,qtd->qcd', placed, normed3).astype(jnp.bfloat16).reshape(-1, D)
        gate_w = lax.dynamic_index_in_dim(w_gate, expert, 0, keepdims=False)
        up_w = lax.dynamic_index_in_dim(w_up, expert, 0, keepdims=False)
        down_w = lax.dynamic_index_in_dim(w_down, expert, 0, keepdims=False)
        gate_val = jnp.dot(slot_block, gate_w, preferred_element_type=jnp.float32)
        up_val = jnp.dot(slot_block, up_w, preferred_element_type=jnp.float32)
        active = (jax.nn.silu(gate_val) * up_val).astype(jnp.bfloat16)
        result = jnp.zeros((slot_block.shape[0], D), jnp.float32)
        for block in range(N_REQ):
            piece = jnp.dot(active[:, block * quarter:(block + 1) * quarter], down_w[block * quarter:(block + 1) * quarter], preferred_element_type=jnp.float32).astype(jnp.bfloat16)
            piece = lax.optimization_barrier(piece)
            result = result + piece.astype(jnp.float32)
        result = result.reshape(REQS, CAP, D)
        accum = accum + jnp.einsum('qct,qcd->qtd', placed * weight_col[:, None, :], result)
        return (accum, None)
    moe, unused = lax.scan(per_expert, jnp.zeros((REQS, TREE, D), jnp.float32), expert_ids)
    layer_out = (mixed_f.reshape(REQS, TREE, D) + moe).astype(jnp.bfloat16)
    new_pools = jax.vmap(write_rows)(pools, page_table, cache_len, accept_path, accept_count, new_latent)
    return (layer_out, new_pools.reshape(REQS * PAGES_DEV, PAGE, LAT + ROPE))
```

```python
import functools
import math

import jax
import jax.numpy as jnp
from jax import lax
from jax.experimental import pallas as pl
from jax.experimental.pallas import tpu as pltpu
from jax.sharding import PartitionSpec as P

MESH = pl.DeviceIdType.MESH
TOP = 6
TREE = 32
NX = 4
NY = 4
NZ = 8
CHUNKS = 4
F32 = jnp.float32
BF16 = jnp.bfloat16


def ancestry(parent_row):
    count = parent_row.shape[0]
    ident = jnp.eye(count, dtype=jnp.int32)
    linked = (parent_row[:, None] == jnp.arange(count, dtype=jnp.int32)[None, :]).astype(jnp.int32)
    reach = jnp.minimum(ident + linked, 1)
    for sweep in range(count.bit_length()):
        reach = jnp.minimum(jnp.dot(reach, reach), 1)
    return reach


def attend(query_row, page_pool, table_row, length, parent_row, fresh, key_up, value_up):
    count = query_row.shape[0]
    heads = key_up.shape[0]
    nope = key_up.shape[1]
    latent = key_up.shape[2]
    shaped = query_row.reshape(count, heads, -1)
    scale = 1.0 / math.sqrt(shaped.shape[2])
    q_nope = shaped[:, :, :nope]
    q_rope = shaped[:, :, nope:]
    q_latent = jnp.einsum("thn,hnc->thc", q_nope, key_up, preferred_element_type=F32).astype(BF16)
    q_full = jnp.concatenate([q_latent, q_rope], axis=2)
    cache_rows = jnp.take(page_pool, table_row, axis=0).reshape(-1, page_pool.shape[2])
    score_cache = jnp.einsum("thc,kc->thk", q_full, cache_rows, preferred_element_type=F32) * scale
    score_tree = jnp.einsum("thc,jc->thj", q_full, fresh, preferred_element_type=F32) * scale
    live = jnp.arange(cache_rows.shape[0], dtype=jnp.int32) < length
    score_cache = jnp.where(live[None, None, :], score_cache, -1e30)
    score_tree = jnp.where(ancestry(parent_row)[:, None, :] > 0, score_tree, -1e30)
    peak = jnp.maximum(jnp.max(score_cache, axis=2), jnp.max(score_tree, axis=2))[:, :, None]
    exp_cache = jnp.exp(score_cache - peak)
    exp_tree = jnp.exp(score_tree - peak)
    total = jnp.sum(exp_cache, axis=2, keepdims=True) + jnp.sum(exp_tree, axis=2, keepdims=True)
    prob_cache = (exp_cache / total).astype(BF16)
    prob_tree = (exp_tree / total).astype(BF16)
    context = jnp.einsum("thk,kc->thc", prob_cache, cache_rows[:, :latent], preferred_element_type=F32)
    context = context + jnp.einsum("thj,jc->thc", prob_tree, fresh[:, :latent], preferred_element_type=F32)
    context = context.astype(BF16)
    head_out = jnp.einsum("thc,hcv->thv", context, value_up, preferred_element_type=F32).astype(BF16)
    return head_out.reshape(count, -1)


def write_rows(page_pool, table_row, length, path_row, count, fresh):
    pool_len = page_pool.shape[0]
    page_size = page_pool.shape[1]
    pool_ids = jnp.arange(pool_len, dtype=jnp.int32)
    match = table_row[None, :] == pool_ids[:, None]
    logical = jnp.sum(jnp.where(match, pool_ids[None, :], 0), axis=1)
    position = logical[:, None] * page_size + jnp.arange(page_size, dtype=jnp.int32)[None, :]
    offset = position - length
    valid = (offset >= 0) & (offset < count)
    steps = jnp.arange(path_row.shape[0], dtype=jnp.int32)
    tokens = jnp.arange(fresh.shape[0], dtype=jnp.int32)
    by_step = jnp.dot(
        (path_row[:, None] == tokens[None, :]).astype(BF16), fresh, preferred_element_type=F32
    ).astype(BF16)
    pick = (offset.reshape(-1)[:, None] == steps[None, :]).astype(BF16)
    written = jnp.dot(pick, by_step, preferred_element_type=F32).astype(BF16)
    return jnp.where(valid[:, :, None], written.reshape(page_pool.shape), page_pool)


def slot_table(route_row, weight_row, expert_ids, capacity):
    hits = route_row[:, :, None] == expert_ids
    chosen = jnp.sum(hits.astype(jnp.int32), axis=1)
    weight_by = jnp.sum(jnp.where(hits, weight_row[:, :, None], 0.0), axis=1)
    tokens = route_row.shape[0]
    earlier = (jnp.arange(tokens)[:, None] > jnp.arange(tokens)[None, :]).astype(BF16)
    before = jnp.dot(earlier, chosen.astype(BF16), preferred_element_type=F32).astype(jnp.int32)
    chosen_t, before_t, weight_t = chosen.T, before.T, weight_by.T
    slot_ids = jnp.arange(capacity, dtype=jnp.int32)
    placed = (chosen_t[:, None, :] > 0) & (before_t[:, None, :] == slot_ids[None, :, None])
    weighted = jnp.where(placed, weight_t[:, None, :], 0.0)
    both = jnp.concatenate([placed.astype(BF16), weighted.astype(BF16)], axis=2)
    both = jnp.pad(both, ((0, 0), (0, 0), (0, 128 - 2 * tokens)))
    return both.reshape(NZ, -1, 128)


def layer_kernel(
    head_ref, hid_ref, gain_ref, tab_ref, perm_ref, spread_ref, mask_ref,
    oproj_hbm, wg_hbm, wu_hbm, wd_hbm,
    out_ref,
    oproj, wg, wu, wd, heads, po, co, mixed, tabs, sel, wt, tok, ysend, x, accg, accu, act,
    p, a1, a3, bl, br, zz, v, zsend, zrecv,
    w_sem, h_s, h_r, o_s, o_r, t_s, t_r, fz_s, fz_r, fy_s, fy_r, fx_s, fx_r,
    gx_s, gx_r, gy_s, gy_r, gz_s, gz_r,
):
    rx = lax.axis_index("req")
    e = lax.axis_index("exp")
    ez = e // (2 * NY)
    ey = (e // 2) % NY
    ec = e % 2
    width = hid_ref.shape[1]
    cc = width // CHUNKS
    slots = ysend.shape[2]
    rows = x.shape[2]
    half = rows // 2
    tree = hid_ref.shape[0]

    def at_x(k):
        return ((rx + k) % NX, e)

    def at_z(k):
        return (rx, (((ez + k) % NZ) * NY + ey) * 2 + ec)

    def at_y(d):
        return (rx, (ez * NY + (ey + d // 2) % NY) * 2 + (ec + d % 2) % 2)

    def flip_y(d):
        return ((NY - d // 2) % NY) * 2 + d % 2

    weights = [
        pltpu.make_async_copy(oproj_hbm, oproj, w_sem.at[0]),
        pltpu.make_async_copy(wg_hbm, wg, w_sem.at[1]),
        pltpu.make_async_copy(wu_hbm, wu, w_sem.at[2]),
        pltpu.make_async_copy(wd_hbm, wd, w_sem.at[3]),
    ]
    for copy in weights:
        copy.start()

    barrier = pltpu.get_barrier_semaphore()
    partners = (
        [at_x(k) for k in range(1, NX)]
        + [at_y(d) for d in range(1, 2 * NY)]
        + [at_z(k) for k in range(1, NZ)]
    )
    for partner in partners:
        pl.semaphore_signal(barrier, inc=1, device_id=partner, device_id_type=MESH)
    pl.semaphore_wait(barrier, len(partners))

    started = []

    def send(src, dst, ss, rs, device):
        copy = pltpu.make_async_remote_copy(
            src_ref=src, dst_ref=dst, send_sem=ss, recv_sem=rs, device_id=device, device_id_type=MESH
        )
        copy.start()
        started.append(copy)
        return copy

    head_copies = [
        send(head_ref, heads.at[NX - k], h_s.at[k], h_r.at[NX - k], at_x(k)) for k in (1, 3, 2)
    ]
    tab_copies = [
        send(tab_ref.at[k], tabs.at[NZ - k], t_s.at[k], t_r.at[NZ - k], at_z(k)) for k in range(1, NZ)
    ]
    heads[0] = head_ref[...]
    tabs[0] = tab_ref[0]
    weights[0].wait()
    for copy in head_copies:
        copy.wait_recv()
    proj = jnp.dot(heads[...].reshape(NX * tree, width), oproj[...], preferred_element_type=F32)
    po[...] = proj.astype(BF16).reshape(po.shape)
    back_copies = [send(po.at[k], co.at[rx], o_s.at[k], o_r.at[NX - k], at_x(k)) for k in (1, 3, 2)]
    co[rx] = po[0]
    for copy in tab_copies:
        copy.wait_recv()
    flat_tabs = tabs[...].reshape(NZ * slots, 128)
    wide = jnp.dot(flat_tabs, spread_ref[...], preferred_element_type=F32) * mask_ref[...].astype(F32)
    both = jnp.dot(perm_ref[...], wide.astype(BF16), preferred_element_type=F32)
    sel[...] = both[:, : NZ * tree].astype(BF16)
    wt[...] = both[:, NZ * tree :].T.astype(BF16)

    for copy in back_copies:
        copy.wait_recv()
    square = jnp.zeros((tree, 1), F32)
    for c in range(CHUNKS):
        m = (hid_ref[:, c * cc : (c + 1) * cc].astype(F32) + co[c].astype(F32)).astype(BF16)
        mixed[c] = m
        mf = m.astype(F32)
        square = square + jnp.sum(mf * mf, axis=1, keepdims=True)
    factor = lax.rsqrt(square * (1.0 / width) + 1e-06)

    fz, fy, fx, fw = {}, {}, {}, {}
    for c in range(CHUNKS):
        gain = gain_ref[:, c * cc : (c + 1) * cc].astype(F32)
        tok[c, 0] = (mixed[c].astype(F32) * factor * gain).astype(BF16)
        fz[c] = [
            send(tok.at[c, 0], tok.at[c, NZ - k], fz_s.at[c, k], fz_r.at[c, NZ - k], at_z(k))
            for k in (1, 7, 2, 6, 3, 5, 4)
        ]

    def select(c):
        for copy in fz[c]:
            copy.wait_recv()
        block = jnp.dot(sel[...], tok[c].reshape(NZ * tree, cc), preferred_element_type=F32)
        block = block.astype(BF16)
        x[c, 0, 0:slots] = block[0:slots]
        ysend[c] = block.reshape(2 * NY, slots, cc)
        fy[c] = [
            send(
                ysend.at[c, d],
                x.at[c, 0, pl.ds(flip_y(d) * slots, slots)],
                fy_s.at[c, d],
                fy_r.at[c, flip_y(d)],
                at_y(d),
            )
            for d in (1, 2, 6, 3, 7, 4, 5)
        ]

    def spread_x(c):
        for copy in fy[c]:
            copy.wait_recv()
        fx[c] = [
            send(x.at[c, 0], x.at[c, 3], fx_s.at[c, 0], fx_r.at[c, 0], at_x(1)),
            send(x.at[c, 0], x.at[c, 1], fx_s.at[c, 1], fx_r.at[c, 1], at_x(3)),
        ]

    def forward_x(c):
        top, bottom = pl.ds(0, half), pl.ds(half, half)
        fx[c][0].wait_recv()
        first = send(x.at[c, 3, top], x.at[c, 2, top], fx_s.at[c, 2], fx_r.at[c, 2], at_x(1))
        fx[c][1].wait_recv()
        second = send(x.at[c, 1, bottom], x.at[c, 2, bottom], fx_s.at[c, 3], fx_r.at[c, 3], at_x(3))
        fw[c] = [first, second]

    def expand(c):
        for copy in fw[c]:
            copy.wait_recv()
        if c == 0:
            weights[1].wait()
            weights[2].wait()

        def body(g, carry):
            block = x[c, g]
            gv = jnp.dot(block, wg[c * cc : (c + 1) * cc, :], preferred_element_type=F32)
            uv = jnp.dot(block, wu[c * cc : (c + 1) * cc, :], preferred_element_type=F32)
            if c > 0:
                gv = gv + accg[g]
                uv = uv + accu[g]
            if c == CHUNKS - 1:
                act[g] = (gv * jax.nn.sigmoid(gv) * uv).astype(BF16)
            else:
                accg[g] = gv
                accu[g] = uv
            return carry

        lax.fori_loop(0, NX, body, 0)

    for i in range(CHUNKS + 3):
        if i < CHUNKS:
            select(i)
        if 0 <= i - 1 < CHUNKS:
            spread_x(i - 1)
        if 0 <= i - 2 < CHUNKS:
            forward_x(i - 2)
        if 0 <= i - 3 < CHUNKS:
            expand(i - 3)

    weights[3].wait()
    gx, gw, gy, gz = {}, {}, {}, {}

    def contract(c):
        top, bottom = pl.ds(0, half), pl.ds(half, half)
        down = wd[:, c * cc : (c + 1) * cc]
        p[c, 2] = jnp.dot(act[2], down, preferred_element_type=F32).astype(BF16)
        gx[c] = [
            send(p.at[c, 2, top], a1.at[c], gx_s.at[c, 0], gx_r.at[c, 0], at_x(1)),
            send(p.at[c, 2, bottom], a3.at[c], gx_s.at[c, 1], gx_r.at[c, 1], at_x(3)),
        ]

        def body(j, carry):
            g = (3 + j) % NX
            down = wd[:, c * cc : (c + 1) * cc]
            p[c, g] = jnp.dot(act[g], down, preferred_element_type=F32).astype(BF16)
            return carry

        lax.fori_loop(0, 3, body, 0)

    def gather_x(c):
        gx[c][0].wait_recv()
        p[c, 1, 0:half] = (p[c, 1, 0:half].astype(F32) + a1[c].astype(F32)).astype(BF16)
        first = send(p.at[c, 1], bl.at[c], gx_s.at[c, 2], gx_r.at[c, 2], at_x(1))
        gx[c][1].wait_recv()
        p[c, 3, half:rows] = (p[c, 3, half:rows].astype(F32) + a3[c].astype(F32)).astype(BF16)
        second = send(p.at[c, 3], br.at[c], gx_s.at[c, 3], gx_r.at[c, 3], at_x(3))
        gw[c] = [first, second]

    def back_y(c):
        for copy in gw[c]:
            copy.wait_recv()
        total = p[c, 0].astype(F32) + bl[c].astype(F32) + br[c].astype(F32)
        total = total.astype(BF16).reshape(2 * NY, slots, cc)
        v[c, 0] = total[0]
        zz[c] = total
        gy[c] = [
            send(zz.at[c, d], v.at[c, flip_y(d)], gy_s.at[c, d], gy_r.at[c, flip_y(d)], at_y(d))
            for d in (1, 2, 6, 3, 7, 4, 5)
        ]

    def back_z(c):
        for copy in gy[c]:
            copy.wait_recv()
        part = jnp.dot(wt[...], v[c].reshape(rows, cc), preferred_element_type=F32)
        zsend[c] = part.astype(BF16).reshape(NZ, tree, cc)
        gz[c] = [
            send(zsend.at[c, k], zrecv.at[c, NZ - k], gz_s.at[c, k], gz_r.at[c, NZ - k], at_z(k))
            for k in (1, 7, 2, 6, 3, 5, 4)
        ]

    def finish(c):
        for copy in gz[c]:
            copy.wait_recv()
        total = mixed[c].astype(F32) + zsend[c, 0].astype(F32)
        for k in range(1, NZ):
            total = total + zrecv[c, k].astype(F32)
        out_ref[:, c * cc : (c + 1) * cc] = total.astype(BF16)

    for i in range(CHUNKS + 4):
        if i < CHUNKS:
            contract(i)
        if 0 <= i - 1 < CHUNKS:
            gather_x(i - 1)
        if 0 <= i - 2 < CHUNKS:
            back_y(i - 2)
        if 0 <= i - 3 < CHUNKS:
            back_z(i - 3)
        if 0 <= i - 4 < CHUNKS:
            finish(i - 4)

    for copy in started:
        copy.wait_send()


def run_layer(head_out, hidden, gain, table, out_proj, w_gate, w_up, w_down):
    tree, width = hidden.shape
    cc = width // CHUNKS
    hid = w_gate.shape[1]
    slots = table.shape[1]
    rows = NZ * slots
    cols = NZ * tree
    i = jnp.arange(rows, dtype=jnp.int32)
    cap = slots // (2 * NY)
    source = ((i % slots) // cap) * slots + (i // slots) * cap + i % cap
    perm = (source[:, None] == i[None, :]).astype(BF16)
    j = jnp.arange(2 * cols, dtype=jnp.int32)
    lane = jnp.arange(128, dtype=jnp.int32)
    spread = ((j[None, :] // cols) * tree + j[None, :] % tree == lane[:, None]).astype(BF16)
    mask = ((i[:, None] // slots) == ((j[None, :] % cols) // tree)).astype(BF16)
    vmem = pl.BlockSpec(memory_space=pltpu.VMEM)
    hbm = pl.BlockSpec(memory_space=pl.ANY)
    dma = pltpu.SemaphoreType.DMA
    c = CHUNKS
    return pl.pallas_call(
        layer_kernel,
        out_shape=jax.ShapeDtypeStruct((tree, width), BF16),
        in_specs=[vmem] * 7 + [hbm] * 4,
        out_specs=vmem,
        scratch_shapes=[
            pltpu.VMEM(out_proj.shape, BF16),
            pltpu.VMEM(w_gate.shape, BF16),
            pltpu.VMEM(w_up.shape, BF16),
            pltpu.VMEM(w_down.shape, BF16),
            pltpu.VMEM((NX, tree, width), BF16),
            pltpu.VMEM((NX, tree, width // NX), BF16),
            pltpu.VMEM((NX, tree, width // NX), BF16),
            pltpu.VMEM((c, tree, cc), BF16),
            pltpu.VMEM((NZ, slots, 128), BF16),
            pltpu.VMEM((rows, cols), BF16),
            pltpu.VMEM((cols, rows), BF16),
            pltpu.VMEM((c, NZ, tree, cc), BF16),
            pltpu.VMEM((c, 2 * NY, slots, cc), BF16),
            pltpu.VMEM((c, NX, rows, cc), BF16),
            pltpu.VMEM((NX, rows, hid), F32),
            pltpu.VMEM((NX, rows, hid), F32),
            pltpu.VMEM((NX, rows, hid), BF16),
            pltpu.VMEM((c, NX, rows, cc), BF16),
            pltpu.VMEM((c, rows // 2, cc), BF16),
            pltpu.VMEM((c, rows // 2, cc), BF16),
            pltpu.VMEM((c, rows, cc), BF16),
            pltpu.VMEM((c, rows, cc), BF16),
            pltpu.VMEM((c, 2 * NY, slots, cc), BF16),
            pltpu.VMEM((c, 2 * NY, slots, cc), BF16),
            pltpu.VMEM((c, NZ, tree, cc), BF16),
            pltpu.VMEM((c, NZ, tree, cc), BF16),
            dma((4,)),
            dma((NX,)), dma((NX,)), dma((NX,)), dma((NX,)),
            dma((NZ,)), dma((NZ,)),
            dma((c, NZ)), dma((c, NZ)), dma((c, 2 * NY)), dma((c, 2 * NY)),
            dma((c, 4)), dma((c, 4)), dma((c, 4)), dma((c, 4)),
            dma((c, 2 * NY)), dma((c, 2 * NY)), dma((c, NZ)), dma((c, NZ)),
        ],
        compiler_params=pltpu.CompilerParams(
            collective_id=0, has_side_effects=True, vmem_limit_bytes=60 * 1024 * 1024
        ),
        name="layer",
    )(head_out, hidden, gain, table, perm, spread, mask, out_proj, w_gate, w_up, w_down)


def local(
    hidden, queries, new_latent, pages, page_table, cache_len, parents, accept_path, accept_count,
    key_up, value_up, out_proj, norm_gain, route_ids, route_weights, w_gate, w_up, w_down,
):
    rx = lax.axis_index("req")
    e = lax.axis_index("exp")
    experts = lax.axis_size("exp") * w_gate.shape[0]
    capacity = max(2, min(TREE, 2 * TREE * TOP // experts))
    order = jnp.arange(experts, dtype=jnp.int32)
    expert_ids = (
        ((e // (2 * NY) + order // (2 * NY)) % NZ) * (2 * NY)
        + ((e // 2 + order // 2) % NY) * 2
        + (e + order) % 2
    )
    ids = lax.dynamic_index_in_dim(route_ids[:, 0], rx, 0, keepdims=False)
    wts = lax.dynamic_index_in_dim(route_weights[:, 0], rx, 0, keepdims=False)
    table = slot_table(ids, wts, expert_ids, capacity)
    head_out = attend(
        queries[0], pages, page_table[0], cache_len[0], parents[0], new_latent[0], key_up, value_up
    )
    layer_out = run_layer(
        head_out, hidden[0], norm_gain[None], table, out_proj, w_gate[0], w_up[0], w_down[0]
    )
    new_pool = write_rows(
        pages, page_table[0], cache_len[0], accept_path[0], accept_count[0], new_latent[0]
    )
    return (layer_out[None], new_pool)


def solution(mesh):
    in_specs = (
        P(("req", "exp"), None, None),
        P(("req", "exp"), None, None),
        P(("req", "exp"), None, None),
        P(("req", "exp"), None, None),
        P(("req", "exp"), None),
        P(("req", "exp")),
        P(("req", "exp"), None),
        P(("req", "exp"), None),
        P(("req", "exp")),
        P(),
        P(),
        P(None, "req"),
        P(),
        P(None, "exp", None, None),
        P(None, "exp", None, None),
        P("exp", None, "req"),
        P("exp", None, "req"),
        P("exp", "req", None),
    )
    out_specs = (P(("req", "exp"), None, None), P(("req", "exp"), None, None))
    return jax.shard_map(local, mesh=mesh, in_specs=in_specs, out_specs=out_specs, check_vma=False)
```

```python
import math

import jax
import jax.numpy as jnp
import numpy as np
from jax import lax
from jax.experimental import pallas as pl
from jax.experimental.pallas import tpu as pltpu
from jax.sharding import PartitionSpec as P

MESH = pl.DeviceIdType.MESH
NX = 4
NY = 4
NZ = 8
CHUNKS = 8
F32 = jnp.float32
BF16 = jnp.bfloat16


def dot(a, b, contract=((1,), (0,))):
    return lax.dot_general(a, b, (contract, ((), ())), preferred_element_type=F32)


def build_table(tab, ids, weights, rep_ref, slot_ref, ez, ey, ec):
    top, tree = ids.shape
    n = NZ * NY * 2
    order = lax.broadcasted_iota(jnp.int32, (n, 1), 0)
    expert = (
        ((ez + (order >> 3)) & 7) * 8 + ((ey + ((order >> 1) & 3)) & 3) * 2 + ((ec + order) & 1)
    )
    chosen = jnp.zeros((n, tree), F32)
    weight = jnp.zeros((n, tree), F32)
    for k in range(top):
        hit = ids[k : k + 1, :] == expert
        chosen = chosen + jnp.where(hit, 1.0, 0.0)
        weight = weight + jnp.where(hit, weights[k : k + 1, :], 0.0)
    one = lax.broadcasted_iota(jnp.int32, (tree, tree), 0)
    two = lax.broadcasted_iota(jnp.int32, (tree, tree), 1)
    earlier = jnp.where(one < two, 1.0, 0.0).astype(BF16)
    before = dot(chosen.astype(BF16), earlier)
    rep = rep_ref[...]
    taken = dot(rep, chosen.astype(BF16))
    rank = dot(rep, before.astype(BF16))
    amount = dot(rep, weight.astype(BF16))
    placed = jnp.logical_and(taken > 0.5, rank == slot_ref[...])
    tab[...] = jnp.zeros(tab.shape, BF16)
    shape = (tab.shape[0], tab.shape[1], tree)
    tab[:, :, 0:tree] = jnp.where(placed, 1.0, 0.0).astype(BF16).reshape(shape)
    tab[:, :, tree : 2 * tree] = jnp.where(placed, amount, 0.0).astype(BF16).reshape(shape)


def ancestors(parents, tree):
    one = lax.broadcasted_iota(jnp.int32, (tree, tree), 0)
    two = lax.broadcasted_iota(jnp.int32, (tree, tree), 1)
    reach = jnp.where(jnp.logical_or(one == parents, one == two), 1.0, 0.0)
    for sweep in range((tree - 1).bit_length()):
        half = reach.astype(BF16)
        reach = jnp.minimum(dot(half, half), 1.0)
    return reach.T


def attend(q_ref, fresh_ref, kt, ku, vu, qs, ctx, heads, live, reach, ku_in, kt_in, vu_in):
    n_heads, nope, latent = ku.shape
    tree = q_ref.shape[0]
    per = q_ref.shape[1] // n_heads
    scale = 1.0 / math.sqrt(per)
    ku_in.wait()
    for h in range(n_heads):
        rows = pl.ds(h * tree, tree)
        q_nope = q_ref[:, h * per : h * per + nope]
        qs[rows, 0:latent] = dot(q_nope, ku[h]).astype(BF16)
        qs[rows, latent:] = q_ref[:, h * per + nope : (h + 1) * per]
    kt_in.wait()
    block = 128
    pairs = kt.shape[0] // 2
    page = kt.shape[2]
    fresh = fresh_ref[...]
    allowed = jnp.concatenate([reach] * (block // tree), axis=0) > 0.5

    def body(i, carry):
        at = pl.multiple_of(i * block, block)
        q = qs[pl.ds(at, block), :]
        tree_score = jnp.where(allowed, dot(q, fresh, ((1,), (1,))) * scale, -1e30)
        scores = []
        for j in range(pairs):
            keys = jnp.concatenate([kt[2 * j], kt[2 * j + 1]], axis=1)
            mask = live[:, 2 * j * page : 2 * (j + 1) * page]
            scores.append(jnp.where(mask, dot(q, keys) * scale, -1e30))
        peak = jnp.max(tree_score, axis=1, keepdims=True)
        for s in scores:
            peak = jnp.maximum(peak, jnp.max(s, axis=1, keepdims=True))
        tree_score = jnp.exp(tree_score - peak)
        scores = [jnp.exp(s - peak) for s in scores]
        total = jnp.sum(tree_score, axis=1, keepdims=True)
        for s in scores:
            total = total + jnp.sum(s, axis=1, keepdims=True)
        inverse = 1.0 / total
        context = dot((tree_score * inverse).astype(BF16), fresh[:, 0:latent])
        for j in range(pairs):
            keys = jnp.concatenate([kt[2 * j, 0:latent], kt[2 * j + 1, 0:latent]], axis=1)
            context = context + dot((scores[j] * inverse).astype(BF16), keys, ((1,), (1,)))
        ctx[pl.ds(at, block), :] = context.astype(BF16)
        return carry

    lax.fori_loop(0, n_heads * tree // block, body, 0)
    vu_in.wait()
    for h in range(n_heads):
        out = dot(ctx[pl.ds(h * tree, tree), :], vu[h])
        heads[0, :, h * vu.shape[2] : (h + 1) * vu.shape[2]] = out.astype(BF16)


def write_pages(kt, fresh_ref, path, offset, count):
    steps = fresh_ref.shape[0]
    step = lax.broadcasted_iota(jnp.int32, (steps, 1), 0)
    by_step = jnp.where(step == path, 1.0, 0.0).astype(BF16)
    page = kt.shape[2]
    for j in range(kt.shape[0]):
        here = offset[:, j * page : (j + 1) * page]
        at_step = jnp.where(step == here, 1.0, 0.0).astype(BF16)
        pick = dot(by_step, at_step).astype(BF16)
        rows = dot(fresh_ref[...], pick, ((0,), (0,))).astype(BF16)
        valid = jnp.where(jnp.logical_and(here >= 0, here < count), 1.0, 0.0)
        old = kt[j]
        kt[j] = jnp.where(jnp.broadcast_to(valid, old.shape) > 0.5, rows.astype(F32), old.astype(F32)).astype(BF16)


def layer_kernel(
    ptab_ref, clen_ref, count_ref,
    hid_ref, q_ref, fresh_ref, parent_ref, path_ref, gain_ref, ids_ref, rw_ref,
    rep_ref, slot_ref, perm_ref, spread_ref, mask_ref,
    pages_hbm, ku_hbm, vu_hbm, oproj_hbm, wg_hbm, wu_hbm, wd_hbm,
    out_ref, newp_hbm,
    kt, ku, vu, qs, ctx,
    oproj, wg, wu, wd, heads, po, co, mixed, tab, tabs, sel, wt, tok, ysend, x, accg, accu, act,
    p, a1, a3, bl, br, zz, v, zsend, zrecv,
    w_sem, h_s, h_r, o_s, o_r, t_s, t_r, fz_s, fz_r, fy_s, fy_r, fx_s, fx_r,
    gx_s, gx_r, gy_s, gy_r, gz_s, gz_r,
):
    rx = lax.axis_index("req")
    e = lax.axis_index("exp")
    ez = e // (2 * NY)
    ey = (e // 2) % NY
    ec = e % 2
    width = hid_ref.shape[1]
    cc = width // CHUNKS
    slots = ysend.shape[2]
    rows = x.shape[2]
    half = rows // 2
    tree = hid_ref.shape[0]

    def at_x(k):
        return ((rx + k) % NX, e)

    def at_z(k):
        return (rx, (((ez + k) % NZ) * NY + ey) * 2 + ec)

    def at_y(d):
        return (rx, (ez * NY + (ey + d // 2) % NY) * 2 + (ec + d % 2) % 2)

    def flip_y(d):
        return ((NY - d // 2) % NY) * 2 + d % 2

    in_copies = [
        pltpu.make_async_copy(src, dst, w_sem.at[n])
        for n, (src, dst) in enumerate(
            [(ku_hbm, ku), (pages_hbm, kt), (vu_hbm, vu), (oproj_hbm, oproj), (wg_hbm, wg), (wu_hbm, wu), (wd_hbm, wd)]
        )
    ]
    ku_in, kt_in, vu_in, oproj_in, wg_in, wu_in, wd_in = in_copies
    for copy in in_copies:
        copy.start()

    barrier = pltpu.get_barrier_semaphore()
    partners = (
        [at_x(k) for k in range(1, NX)]
        + [at_y(d) for d in range(1, 2 * NY)]
        + [at_z(k) for k in range(1, NZ)]
    )
    for partner in partners:
        pl.semaphore_signal(barrier, inc=1, device_id=partner, device_id_type=MESH)

    build_table(tab, ids_ref[rx], rw_ref[rx], rep_ref, slot_ref, ez, ey, ec)
    page_len = kt.shape[2]
    n_pages = kt.shape[0]
    lane = lax.broadcasted_iota(jnp.int32, (1, page_len), 1)
    position = []
    for j in range(n_pages):
        logical = jnp.int32(0)
        for k in range(n_pages):
            logical = logical + jnp.where(ptab_ref[0, k] == j, k, 0)
        position.append(logical * page_len + lane)
    position = jnp.concatenate(position, axis=1)
    length = clen_ref[0]
    reach = ancestors(parent_ref[...], tree)

    pl.semaphore_wait(barrier, len(partners))

    started = []

    def send(src, dst, ss, rs, device):
        copy = pltpu.make_async_remote_copy(
            src_ref=src, dst_ref=dst, send_sem=ss, recv_sem=rs, device_id=device, device_id_type=MESH
        )
        copy.start()
        started.append(copy)
        return copy

    tabs[0] = tab[0]
    tab_copies = [send(tab.at[k], tabs.at[NZ - k], t_s.at[k], t_r.at[NZ - k], at_z(k)) for k in range(1, NZ)]

    attend(q_ref, fresh_ref, kt, ku, vu, qs, ctx, heads, position < length, reach, ku_in, kt_in, vu_in)
    head_copies = [
        send(heads.at[0], heads.at[NX - k], h_s.at[k], h_r.at[NX - k], at_x(k)) for k in (1, 3, 2)
    ]
    for copy in tab_copies:
        copy.wait_recv()
    flat_tabs = tabs[...].reshape(NZ * slots, 128)
    wide = dot(flat_tabs, spread_ref[...]) * mask_ref[...].astype(F32)
    both = dot(perm_ref[...], wide.astype(BF16))
    sel[...] = both[:, : NZ * tree].astype(BF16)
    wt[...] = both[:, NZ * tree :].T.astype(BF16)

    oproj_in.wait()
    for copy in head_copies:
        copy.wait_recv()
    proj = jnp.dot(heads[...].reshape(NX * tree, width), oproj[...], preferred_element_type=F32)
    po[...] = proj.astype(BF16).reshape(po.shape)
    back_copies = [send(po.at[k], co.at[rx], o_s.at[k], o_r.at[NX - k], at_x(k)) for k in (1, 3, 2)]
    co[rx] = po[0]
    for copy in back_copies:
        copy.wait_recv()
    square = jnp.zeros((tree, 1), F32)
    for c in range(CHUNKS):
        per = width // NX
        at = c * cc % per
        column = co[c * cc // per, :, at : at + cc].astype(F32)
        m = (hid_ref[:, c * cc : (c + 1) * cc].astype(F32) + column).astype(BF16)
        mixed[c] = m
        mf = m.astype(F32)
        square = square + jnp.sum(mf * mf, axis=1, keepdims=True)
    factor = lax.rsqrt(square * (1.0 / width) + 1e-06)

    fz, fy, fx, fw = {}, {}, {}, {}
    for c in range(CHUNKS):
        gain = gain_ref[:, c * cc : (c + 1) * cc].astype(F32)
        tok[c, 0] = (mixed[c].astype(F32) * factor * gain).astype(BF16)
        fz[c] = [
            send(tok.at[c, 0], tok.at[c, NZ - k], fz_s.at[c, k], fz_r.at[c, NZ - k], at_z(k))
            for k in (1, 7, 2, 6, 3, 5, 4)
        ]

    def select(c):
        for copy in fz[c]:
            copy.wait_recv()
        block = jnp.dot(sel[...], tok[c].reshape(NZ * tree, cc), preferred_element_type=F32)
        block = block.astype(BF16)
        x[c, 0, 0:slots] = block[0:slots]
        ysend[c] = block.reshape(2 * NY, slots, cc)
        fy[c] = [
            send(
                ysend.at[c, d],
                x.at[c, 0, pl.ds(flip_y(d) * slots, slots)],
                fy_s.at[c, d],
                fy_r.at[c, flip_y(d)],
                at_y(d),
            )
            for d in (1, 2, 6, 3, 7, 4, 5)
        ]

    def spread_x(c):
        for copy in fy[c]:
            copy.wait_recv()
        fx[c] = [
            send(x.at[c, 0], x.at[c, 3], fx_s.at[c, 0], fx_r.at[c, 0], at_x(1)),
            send(x.at[c, 0], x.at[c, 1], fx_s.at[c, 1], fx_r.at[c, 1], at_x(3)),
        ]

    def forward_x(c):
        top, bottom = pl.ds(0, half), pl.ds(half, half)
        fx[c][0].wait_recv()
        first = send(x.at[c, 3, top], x.at[c, 2, top], fx_s.at[c, 2], fx_r.at[c, 2], at_x(1))
        fx[c][1].wait_recv()
        second = send(x.at[c, 1, bottom], x.at[c, 2, bottom], fx_s.at[c, 3], fx_r.at[c, 3], at_x(3))
        fw[c] = [first, second]

    def expand(c):
        for copy in fw[c]:
            copy.wait_recv()
        if c == 0:
            wg_in.wait()
            wu_in.wait()

        def body(g, carry):
            block = x[c, g]
            gv = dot(block, wg[:, c * cc : (c + 1) * cc], ((1,), (1,)))
            uv = dot(block, wu[:, c * cc : (c + 1) * cc], ((1,), (1,)))
            if c > 0:
                gv = gv + accg[g]
                uv = uv + accu[g]
            if c == CHUNKS - 1:
                act[g] = (gv * jax.nn.sigmoid(gv) * uv).astype(BF16)
            else:
                accg[g] = gv
                accu[g] = uv
            return carry

        lax.fori_loop(0, NX, body, 0)

    for i in range(CHUNKS + 3):
        if i < CHUNKS:
            select(i)
        if 0 <= i - 1 < CHUNKS:
            spread_x(i - 1)
        if 0 <= i - 2 < CHUNKS:
            forward_x(i - 2)
        if 0 <= i - 3 < CHUNKS:
            expand(i - 3)
        if i == 2:
            write_pages(kt, fresh_ref, path_ref[...], position - length, count_ref[0])
            page_out = pltpu.make_async_copy(kt, newp_hbm, w_sem.at[7])
            page_out.start()

    wd_in.wait()
    gx, gw, gy, gz = {}, {}, {}, {}

    def contract(c):
        top, bottom = pl.ds(0, half), pl.ds(half, half)
        down = wd[:, c * cc : (c + 1) * cc]
        p[c, 2] = jnp.dot(act[2], down, preferred_element_type=F32).astype(BF16)
        gx[c] = [
            send(p.at[c, 2, top], a1.at[c], gx_s.at[c, 0], gx_r.at[c, 0], at_x(1)),
            send(p.at[c, 2, bottom], a3.at[c], gx_s.at[c, 1], gx_r.at[c, 1], at_x(3)),
        ]

        def body(j, carry):
            g = (3 + j) % NX
            down = wd[:, c * cc : (c + 1) * cc]
            p[c, g] = jnp.dot(act[g], down, preferred_element_type=F32).astype(BF16)
            return carry

        lax.fori_loop(0, 3, body, 0)

    def gather_x(c):
        gx[c][0].wait_recv()
        p[c, 1, 0:half] = (p[c, 1, 0:half].astype(F32) + a1[c].astype(F32)).astype(BF16)
        first = send(p.at[c, 1], bl.at[c], gx_s.at[c, 2], gx_r.at[c, 2], at_x(1))
        gx[c][1].wait_recv()
        p[c, 3, half:rows] = (p[c, 3, half:rows].astype(F32) + a3[c].astype(F32)).astype(BF16)
        second = send(p.at[c, 3], br.at[c], gx_s.at[c, 3], gx_r.at[c, 3], at_x(3))
        gw[c] = [first, second]

    def back_y(c):
        for copy in gw[c]:
            copy.wait_recv()
        total = p[c, 0].astype(F32) + bl[c].astype(F32) + br[c].astype(F32)
        total = total.astype(BF16).reshape(2 * NY, slots, cc)
        v[c, 0] = total[0]
        zz[c] = total
        gy[c] = [
            send(zz.at[c, d], v.at[c, flip_y(d)], gy_s.at[c, d], gy_r.at[c, flip_y(d)], at_y(d))
            for d in (1, 2, 6, 3, 7, 4, 5)
        ]

    def back_z(c):
        for copy in gy[c]:
            copy.wait_recv()
        part = jnp.dot(wt[...], v[c].reshape(rows, cc), preferred_element_type=F32)
        zsend[c] = part.astype(BF16).reshape(NZ, tree, cc)
        gz[c] = [
            send(zsend.at[c, k], zrecv.at[c, NZ - k], gz_s.at[c, k], gz_r.at[c, NZ - k], at_z(k))
            for k in (1, 7, 2, 6, 3, 5, 4)
        ]

    def finish(c):
        for copy in gz[c]:
            copy.wait_recv()
        total = mixed[c].astype(F32) + zsend[c, 0].astype(F32)
        for k in range(1, NZ):
            total = total + zrecv[c, k].astype(F32)
        out_ref[:, c * cc : (c + 1) * cc] = total.astype(BF16)

    for i in range(CHUNKS + 4):
        if i < CHUNKS:
            contract(i)
        if 0 <= i - 1 < CHUNKS:
            gather_x(i - 1)
        if 0 <= i - 2 < CHUNKS:
            back_y(i - 2)
        if 0 <= i - 3 < CHUNKS:
            back_z(i - 3)
        if 0 <= i - 4 < CHUNKS:
            finish(i - 4)

    for copy in started:
        copy.wait_send()
    page_out.wait()


def constants(tree, cap):
    slots = 2 * NY * cap
    rows, cols = NZ * slots, NZ * tree
    i = np.arange(rows)
    source = ((i % slots) // cap) * slots + (i // slots) * cap + i % cap
    perm = source[:, None] == i[None, :]
    j = np.arange(2 * cols)
    lane = np.arange(128)
    spread = (j[None, :] // cols) * tree + j[None, :] % tree == lane[:, None]
    mask = (i[:, None] // slots) == ((j[None, :] % cols) // tree)
    rep = i[:, None] // cap == np.arange(rows // cap)[None, :]
    slot = (i % cap)[:, None].astype(np.float32)
    return [rep.astype(BF16), slot, perm.astype(BF16), spread.astype(BF16), mask.astype(BF16)]


def run_layer(
    hidden, queries, fresh, pages_t, page_table, cache_len, parents, accept_path, accept_count,
    key_up, value_up, out_proj, gain, ids, weights, wg_t, wu_t, w_down,
):
    tree, width = hidden.shape
    cc = width // CHUNKS
    hid = w_down.shape[0]
    n_heads = key_up.shape[0]
    cap = max(2, min(tree, 2 * tree * ids.shape[1] // (NZ * NY * 2)))
    slots = 2 * NY * cap
    rows = NZ * slots
    cols = NZ * tree
    smem = pl.BlockSpec(memory_space=pltpu.SMEM)
    vmem = pl.BlockSpec(memory_space=pltpu.VMEM)
    hbm = pl.BlockSpec(memory_space=pl.ANY)
    dma = pltpu.SemaphoreType.DMA
    c = CHUNKS
    return pl.pallas_call(
        layer_kernel,
        out_shape=(jax.ShapeDtypeStruct((tree, width), BF16), jax.ShapeDtypeStruct(pages_t.shape, BF16)),
        in_specs=[smem] * 3 + [vmem] * 13 + [hbm] * 7,
        out_specs=(vmem, hbm),
        scratch_shapes=[
            pltpu.VMEM(pages_t.shape, BF16),
            pltpu.VMEM(key_up.shape, BF16),
            pltpu.VMEM(value_up.shape, BF16),
            pltpu.VMEM((n_heads * tree, fresh.shape[1]), BF16),
            pltpu.VMEM((n_heads * tree, key_up.shape[2]), BF16),
            pltpu.VMEM(out_proj.shape, BF16),
            pltpu.VMEM(wg_t.shape, BF16),
            pltpu.VMEM(wu_t.shape, BF16),
            pltpu.VMEM(w_down.shape, BF16),
            pltpu.VMEM((NX, tree, width), BF16),
            pltpu.VMEM((NX, tree, width // NX), BF16),
            pltpu.VMEM((NX, tree, width // NX), BF16),
            pltpu.VMEM((c, tree, cc), BF16),
            pltpu.VMEM((NZ, slots, 128), BF16),
            pltpu.VMEM((NZ, slots, 128), BF16),
            pltpu.VMEM((rows, cols), BF16),
            pltpu.VMEM((cols, rows), BF16),
            pltpu.VMEM((c, NZ, tree, cc), BF16),
            pltpu.VMEM((c, 2 * NY, slots, cc), BF16),
            pltpu.VMEM((c, NX, rows, cc), BF16),
            pltpu.VMEM((NX, rows, hid), F32),
            pltpu.VMEM((NX, rows, hid), F32),
            pltpu.VMEM((NX, rows, hid), BF16),
            pltpu.VMEM((c, NX, rows, cc), BF16),
            pltpu.VMEM((c, rows // 2, cc), BF16),
            pltpu.VMEM((c, rows // 2, cc), BF16),
            pltpu.VMEM((c, rows, cc), BF16),
            pltpu.VMEM((c, rows, cc), BF16),
            pltpu.VMEM((c, 2 * NY, slots, cc), BF16),
            pltpu.VMEM((c, 2 * NY, slots, cc), BF16),
            pltpu.VMEM((c, NZ, tree, cc), BF16),
            pltpu.VMEM((c, NZ, tree, cc), BF16),
            dma((8,)),
            dma((NX,)), dma((NX,)), dma((NX,)), dma((NX,)),
            dma((NZ,)), dma((NZ,)),
            dma((c, NZ)), dma((c, NZ)), dma((c, 2 * NY)), dma((c, 2 * NY)),
            dma((c, 4)), dma((c, 4)), dma((c, 4)), dma((c, 4)),
            dma((c, 2 * NY)), dma((c, 2 * NY)), dma((c, NZ)), dma((c, NZ)),
        ],
        compiler_params=pltpu.CompilerParams(
            collective_id=0, has_side_effects=True, vmem_limit_bytes=60 * 1024 * 1024
        ),
        name="layer",
    )(
        page_table, cache_len, accept_count,
        hidden, queries, fresh, parents, accept_path, gain, ids, weights,
        *[jnp.asarray(value) for value in constants(tree, cap)],
        pages_t, key_up, value_up, out_proj, wg_t, wu_t, w_down,
    )


def local(
    hidden, queries, new_latent, pages, page_table, cache_len, parents, accept_path, accept_count,
    key_up, value_up, out_proj, norm_gain, route_ids, route_weights, w_gate, w_up, w_down,
):
    layer_out, pages_out = run_layer(
        hidden[0], queries[0], new_latent[0], jnp.swapaxes(pages, 1, 2), page_table, cache_len, parents,
        accept_path, accept_count, key_up, value_up, out_proj, norm_gain[None],
        jnp.swapaxes(route_ids[:, 0], 1, 2), jnp.swapaxes(route_weights[:, 0], 1, 2),
        jnp.swapaxes(w_gate[0], 0, 1), jnp.swapaxes(w_up[0], 0, 1), w_down[0],
    )
    return (layer_out[None], jnp.swapaxes(pages_out, 1, 2))


def solution(mesh):
    in_specs = (
        P(("req", "exp"), None, None),
        P(("req", "exp"), None, None),
        P(("req", "exp"), None, None),
        P(("req", "exp"), None, None),
        P(("req", "exp"), None),
        P(("req", "exp")),
        P(("req", "exp"), None),
        P(("req", "exp"), None),
        P(("req", "exp")),
        P(),
        P(),
        P(None, "req"),
        P(),
        P(None, "exp", None, None),
        P(None, "exp", None, None),
        P("exp", None, "req"),
        P("exp", None, "req"),
        P("exp", "req", None),
    )
    out_specs = (P(("req", "exp"), None, None), P(("req", "exp"), None, None))
    return jax.shard_map(local, mesh=mesh, in_specs=in_specs, out_specs=out_specs, check_vma=False)
```

```python
import math

import jax
import jax.numpy as jnp
import numpy as np
from jax import lax
from jax.experimental import pallas as pl
from jax.experimental.pallas import tpu as pltpu
from jax.sharding import PartitionSpec as P

MESH = pl.DeviceIdType.MESH
NX = 4
NY = 4
NZ = 8
CHUNKS = 8
EARLY = 2
LATE = CHUNKS - EARLY
EARLY_Z_AT = (0, 1)
EARLY_RELAY_AT = (2, 3)
SELECT_AT = (4, 5)
EXPAND_AT = (6, 8)
CONTRACT_AT = (0, 1)
BACK_Z_AT = (2, 4)
BACK_RELAY_AT = (3, 5)
BACK_X_AT = (5, 7)
F32 = jnp.float32
BF16 = jnp.bfloat16


def dot(a, b, contract=((1,), (0,))):
    return lax.dot_general(a, b, (contract, ((), ())), preferred_element_type=F32)


def pack_routes(ids_ref, weights_ref, rx):
    top, tree = ids_ref.shape[1], ids_ref.shape[3]
    ids = jnp.concatenate([ids_ref[rx, k].astype(F32) for k in range(top)], axis=0)
    weights = jnp.concatenate([weights_ref[rx, k] for k in range(top)], axis=0)
    both = jnp.concatenate([ids, weights, jnp.zeros((top, 128 - 2 * tree), F32)], axis=1)
    return jnp.concatenate([both, jnp.zeros((16 - top, 128), F32)], axis=0).astype(BF16)


def selection(routes, g, top, tree, const_ref, ez, ey, ec):
    n = routes.shape[0]
    tiles = [routes[k, g].astype(F32) for k in range(n)]
    ids = jnp.concatenate([t[0:top, 0:tree] for t in tiles], axis=1)
    weights = jnp.concatenate([t[0:top, tree : 2 * tree] for t in tiles], axis=1)
    order = lax.broadcasted_iota(jnp.int32, (2 * NY, 1), 0)
    expert = (ez * (2 * NY) + ((ey + (order >> 1)) & 3) * 2 + ((ec + order) & 1)).astype(F32)
    cols = n * tree
    chosen = jnp.zeros((2 * NY, cols), F32)
    weight = jnp.zeros((2 * NY, cols), F32)
    for k in range(top):
        hit = ids[k : k + 1, :] == expert
        chosen = chosen + jnp.where(hit, 1.0, 0.0)
        weight = weight + jnp.where(hit, weights[k : k + 1, :], 0.0)
    one = lax.broadcasted_iota(jnp.int32, (cols, cols), 0)
    two = lax.broadcasted_iota(jnp.int32, (cols, cols), 1)
    earlier = jnp.logical_and((one >> 5) == (two >> 5), one < two)
    before = dot(chosen.astype(BF16), jnp.where(earlier, 1.0, 0.0).astype(BF16))
    which = lax.broadcasted_iota(jnp.int32, (1, 2 * NY), 1)
    copy_rows = jnp.where(const_ref[:, 0:1] == which, 1.0, 0.0).astype(BF16)
    lane = lax.broadcasted_iota(jnp.int32, (1, cols), 1)
    taken = dot(copy_rows, chosen.astype(BF16))
    rank = dot(copy_rows, before.astype(BF16))
    amount = dot(copy_rows, weight.astype(BF16))
    placed = jnp.logical_and(taken > 0.5, rank == const_ref[:, 2:3].astype(F32))
    placed = jnp.logical_and(placed, const_ref[:, 1:2] == (lane >> 5))
    return jnp.where(placed, 1.0, 0.0).astype(BF16), jnp.where(placed, amount, 0.0).T.astype(BF16)


def ancestors(parents, tree):
    one = lax.broadcasted_iota(jnp.int32, (tree, tree), 0)
    two = lax.broadcasted_iota(jnp.int32, (tree, tree), 1)
    reach = jnp.where(jnp.logical_or(one == parents, one == two), 1.0, 0.0)
    for sweep in range((tree - 1).bit_length()):
        half = reach.astype(BF16)
        reach = jnp.minimum(dot(half, half), 1.0)
    return reach.T


def make_queries(q_ref, ku, qs, arriving):
    n_heads, nope, latent = ku.shape
    tree = q_ref.shape[0]
    per = q_ref.shape[1] // n_heads
    for copy in arriving:
        copy.wait()
    for h in range(n_heads):
        rows = pl.ds(h * tree, tree)
        q_nope = q_ref[:, h * per : h * per + nope]
        qs[rows, 0:latent] = dot(q_nope, ku[h]).astype(BF16)
        qs[rows, latent:] = q_ref[:, h * per + nope : (h + 1) * per]


def attend(fresh_ref, kt, vu, qs, ctx, heads, live, reach, arriving):
    n_heads, latent, value = vu.shape
    tree = fresh_ref.shape[0]
    scale = 1.0 / math.sqrt(value + qs.shape[1] - latent)
    for copy in arriving[:2]:
        copy.wait()
    block = 128
    pairs = kt.shape[0] // 2
    page = kt.shape[2]
    fresh = fresh_ref[...]
    allowed = jnp.concatenate([reach] * (block // tree), axis=0) > 0.5

    def body(i, carry):
        at = pl.multiple_of(i * block, block)
        q = qs[pl.ds(at, block), :]
        tree_score = jnp.where(allowed, dot(q, fresh, ((1,), (1,))) * scale, -1e30)
        scores = []
        for j in range(pairs):
            keys = jnp.concatenate([kt[2 * j], kt[2 * j + 1]], axis=1)
            mask = live[:, 2 * j * page : 2 * (j + 1) * page]
            scores.append(jnp.where(mask, dot(q, keys) * scale, -1e30))
        peak = jnp.max(tree_score, axis=1, keepdims=True)
        for s in scores:
            peak = jnp.maximum(peak, jnp.max(s, axis=1, keepdims=True))
        tree_score = jnp.exp(tree_score - peak)
        scores = [jnp.exp(s - peak) for s in scores]
        total = jnp.sum(tree_score, axis=1, keepdims=True)
        for s in scores:
            total = total + jnp.sum(s, axis=1, keepdims=True)
        inverse = 1.0 / total
        context = dot((tree_score * inverse).astype(BF16), fresh[:, 0:latent])
        for j in range(pairs):
            keys = jnp.concatenate([kt[2 * j, 0:latent], kt[2 * j + 1, 0:latent]], axis=1)
            context = context + dot((scores[j] * inverse).astype(BF16), keys, ((1,), (1,)))
        ctx[pl.ds(at, block), :] = context.astype(BF16)
        return carry

    lax.fori_loop(0, n_heads * tree // block, body, 0)
    arriving[2].wait()
    for h in range(n_heads):
        out = dot(ctx[pl.ds(h * tree, tree), :], vu[h])
        heads[0, :, h * vu.shape[2] : (h + 1) * vu.shape[2]] = out.astype(BF16)


def write_pages(kt, fresh_ref, path, offset, count):
    steps = fresh_ref.shape[0]
    step = lax.broadcasted_iota(jnp.int32, (steps, 1), 0)
    by_step = jnp.where(step == path, 1.0, 0.0).astype(BF16)
    page = kt.shape[2]
    for j in range(kt.shape[0]):
        here = offset[:, j * page : (j + 1) * page]
        at_step = jnp.where(step == here, 1.0, 0.0).astype(BF16)
        pick = dot(by_step, at_step).astype(BF16)
        rows = dot(fresh_ref[...], pick, ((0,), (0,))).astype(BF16)
        valid = jnp.where(jnp.logical_and(here >= 0, here < count), 1.0, 0.0)
        old = kt[j]
        kt[j] = jnp.where(jnp.broadcast_to(valid, old.shape) > 0.5, rows.astype(F32), old.astype(F32)).astype(BF16)


def layer_kernel(
    ptab_ref, clen_ref, count_ref,
    hid_hbm, q_hbm, fresh_hbm, parent_hbm, path_hbm, gain_hbm, ids_hbm, rw_hbm, const_hbm,
    pages_hbm, ku_hbm, vu_hbm, oproj_hbm, wg_hbm, wu_hbm, wd_hbm,
    out_ref, newp_hbm,
    hid_ref, q_ref, fresh_ref, parent_ref, path_ref, gain_ref, ids_ref, rw_ref, const_ref,
    kt, ku, vu, oproj, wg, wu, wd,
    qs, ctx, heads, po, co, mixed, routes, sel, wt, tok, ysend, x, accg, accu, act,
    p, a1, a3, bl, br, zz, v, zsend, zrecv,
    etok, eysend, ev, ezsend, ezrecv, exsend, exrecv,
    w_sem, h_s, h_r, o_s, o_r, tx_s, tx_r, t_s, t_r, fz_s, fz_r, fy_s, fy_r, fx_s, fx_r,
    gx_s, gx_r, gy_s, gy_r, gz_s, gz_r,
    efx_s, efx_r, efz_s, efz_r, efy_s, efy_r, egy_s, egy_r, egz_s, egz_r, egx_s, egx_r,
):
    rx = lax.axis_index("req")
    e = lax.axis_index("exp")
    ez = e // (2 * NY)
    ey = (e // 2) % NY
    ec = e % 2
    width = hid_ref.shape[1]
    cc = width // CHUNKS
    slots = ysend.shape[2]
    rows = x.shape[2]
    half = rows // 2
    tree = hid_ref.shape[0]

    def at_x(k):
        return ((rx + k) % NX, e)

    def at_z(k):
        return (rx, (((ez + k) % NZ) * NY + ey) * 2 + ec)

    def at_y(d):
        return (rx, (ez * NY + (ey + d // 2) % NY) * 2 + (ec + d % 2) % 2)

    def flip_y(d):
        return ((NY - d // 2) % NY) * 2 + d % 2

    in_copies = [
        pltpu.make_async_copy(src, dst, w_sem.at[n])
        for n, (src, dst) in enumerate(
            [
                (ids_hbm, ids_ref), (rw_hbm, rw_ref), (const_hbm, const_ref), (parent_hbm, parent_ref),
                (q_hbm, q_ref), (ku_hbm, ku), (pages_hbm, kt), (fresh_hbm, fresh_ref), (vu_hbm, vu),
                (oproj_hbm, oproj), (hid_hbm, hid_ref), (gain_hbm, gain_ref), (path_hbm, path_ref),
                (wg_hbm, wg), (wu_hbm, wu), (wd_hbm, wd),
            ]
        )
    ]
    for copy in in_copies:
        copy.start()
    hid_in, gain_in, path_in, wg_in, wu_in, wd_in = in_copies[10:]

    barrier = pltpu.get_barrier_semaphore()
    partners = (
        [at_x(k) for k in range(1, NX)]
        + [at_y(d) for d in range(1, 2 * NY)]
        + [at_z(k) for k in range(1, NZ)]
    )
    for partner in partners:
        pl.semaphore_signal(barrier, inc=1, device_id=partner, device_id_type=MESH)

    for copy in in_copies[:4]:
        copy.wait()
    routes[0, 0] = pack_routes(ids_ref, rw_ref, rx)
    page_len = kt.shape[2]
    n_pages = kt.shape[0]
    lane = lax.broadcasted_iota(jnp.int32, (1, page_len), 1)
    position = []
    for j in range(n_pages):
        logical = jnp.int32(0)
        for k in range(n_pages):
            logical = logical + jnp.where(ptab_ref[0, k] == j, k, 0)
        position.append(logical * page_len + lane)
    position = jnp.concatenate(position, axis=1)
    length = clen_ref[0]
    reach = ancestors(parent_ref[...], tree)

    started = []

    def send(src, dst, ss, rs, device):
        copy = pltpu.make_async_remote_copy(
            src_ref=src, dst_ref=dst, send_sem=ss, recv_sem=rs, device_id=device, device_id_type=MESH
        )
        copy.start()
        started.append(copy)
        return copy

    make_queries(q_ref, ku, qs, in_copies[4:6])
    attend(fresh_ref, kt, vu, qs, ctx, heads, position < length, reach, in_copies[6:9])
    pl.semaphore_wait(barrier, len(partners))

    route_copies = [
        send(routes.at[0, 0], routes.at[0, NX - k], tx_s.at[k], tx_r.at[NX - k], at_x(k)) for k in (1, 3, 2)
    ]
    head_copies = [
        send(heads.at[0], heads.at[NX - k], h_s.at[k], h_r.at[NX - k], at_x(k)) for k in (1, 3, 2)
    ]
    for copy in route_copies:
        copy.wait_recv()
    route_copies = [
        send(routes.at[0], routes.at[NZ - k], t_s.at[k], t_r.at[NZ - k], at_z(k)) for k in (1, 7, 2, 6, 3, 5, 4)
    ]
    for copy in in_copies[9:12]:
        copy.wait()
    for copy in head_copies:
        copy.wait_recv()
    proj = jnp.dot(heads[...].reshape(NX * tree, width), oproj[...], preferred_element_type=F32)
    po[...] = proj.astype(BF16).reshape(po.shape)
    back_copies = [send(po.at[k], co.at[rx], o_s.at[k], o_r.at[NX - k], at_x(k)) for k in (1, 3, 2)]
    co[rx] = po[0]
    for copy in route_copies:
        copy.wait_recv()

    def choose(g, carry):
        sel[g], wt[g] = selection(routes, g, ids_ref.shape[1], tree, const_ref, ez, ey, ec)
        return carry

    lax.fori_loop(0, NX, choose, 0)
    for copy in back_copies:
        copy.wait_recv()
    square = jnp.zeros((tree, 1), F32)
    for c in range(CHUNKS):
        per = width // NX
        at = c * cc % per
        column = co[c * cc // per, :, at : at + cc].astype(F32)
        m = (hid_ref[:, c * cc : (c + 1) * cc].astype(F32) + column).astype(BF16)
        mixed[c] = m
        mf = m.astype(F32)
        square = square + jnp.sum(mf * mf, axis=1, keepdims=True)
    factor = lax.rsqrt(square * (1.0 / width) + 1e-06)

    fz, fy, fx, fw = {}, {}, {}, {}
    efx, efz, efy = {}, {}, {}

    def normed(c):
        at = c * cc // 128
        gain = jnp.concatenate([gain_ref[n : n + 1, :] for n in range(at, at + cc // 128)], axis=1)
        return (mixed[c].astype(F32) * factor * gain.astype(F32)).astype(BF16)

    for b in range(EARLY):
        etok[b, 0, 0] = normed(LATE + b)
        efx[b] = [
            send(etok.at[b, 0, 0], etok.at[b, 0, NX - k], efx_s.at[b, k], efx_r.at[b, NX - k], at_x(k))
            for k in (1, 3, 2)
        ]

    near, far = (1, 7, 2, 6), (1, 7, 2, 6, 3, 5, 4)
    fr, efr = {}, {}

    def to_z(src, dst, ss, rs, steps):
        return [send(src, dst.at[NZ - k], ss.at[k], rs.at[NZ - k], at_z(k)) for k in steps]

    def relay(ref, ss, rs, copies):
        copies[2].wait_recv()
        copies[3].wait_recv()
        low, high = pl.ds(0, tree // 2), pl.ds(tree // 2, tree // 2)
        if len(ref.shape) == 3:
            parts = [ref.at[6, low], ref.at[4, low], ref.at[2, high], ref.at[4, high]]
        else:
            parts = [ref.at[6, :, low], ref.at[4, :, low], ref.at[2, :, high], ref.at[4, :, high]]
        return copies[:2] + [
            send(ref.at[6], ref.at[5], ss.at[3], rs.at[5], at_z(1)),
            send(ref.at[2], ref.at[3], ss.at[5], rs.at[3], at_z(7)),
            send(parts[0], parts[1], ss.at[4], rs.at[4], at_z(2)),
            send(parts[2], parts[3], ss.at[0], rs.at[0], at_z(6)),
        ]

    def spread_z(c):
        tok[c, 0] = normed(c)
        fz[c] = to_z(tok.at[c, 0], tok.at[c], fz_s.at[c], fz_r.at[c], near if c else far)

    def relay_z(c):
        fz[c] = relay(tok.at[c], fz_s.at[c], fz_r.at[c], fz[c])

    def early_z(b):
        for copy in efx[b]:
            copy.wait_recv()
        efz[b] = to_z(etok.at[b, 0], etok.at[b], efz_s.at[b], efz_r.at[b], near)

    def early_relay(b):
        efz[b] = relay(etok.at[b], efz_s.at[b], efz_r.at[b], efz[b])

    def early_select(b):
        for copy in efz[b]:
            copy.wait_recv()
        c = LATE + b

        def body(g, carry):
            block = dot(sel[g], etok[b, :, g].reshape(NZ * tree, cc)).astype(BF16)
            x[c, g, 0:slots] = block[0:slots]
            eysend[b, :, g] = block.reshape(2 * NY, slots, cc)
            return carry

        lax.fori_loop(0, NX, body, 0)
        efy[b] = [
            send(
                eysend.at[b, d],
                x.at[c, :, pl.ds(flip_y(d) * slots, slots)],
                efy_s.at[b, d],
                efy_r.at[b, flip_y(d)],
                at_y(d),
            )
            for d in (1, 2, 6, 3, 7, 4, 5)
        ]

    def select(c):
        for copy in fz[c]:
            copy.wait_recv()
        block = jnp.dot(sel[0], tok[c].reshape(NZ * tree, cc), preferred_element_type=F32)
        block = block.astype(BF16)
        x[c, 0, 0:slots] = block[0:slots]
        ysend[c] = block.reshape(2 * NY, slots, cc)
        fy[c] = [
            send(
                ysend.at[c, d],
                x.at[c, 0, pl.ds(flip_y(d) * slots, slots)],
                fy_s.at[c, d],
                fy_r.at[c, flip_y(d)],
                at_y(d),
            )
            for d in (1, 2, 6, 3, 7, 4, 5)
        ]

    def spread_x(c):
        for copy in fy[c]:
            copy.wait_recv()
        fx[c] = [
            send(x.at[c, 0], x.at[c, 3], fx_s.at[c, 0], fx_r.at[c, 0], at_x(1)),
            send(x.at[c, 0], x.at[c, 1], fx_s.at[c, 1], fx_r.at[c, 1], at_x(3)),
        ]

    def forward_x(c):
        top, bottom = pl.ds(0, half), pl.ds(half, half)
        fx[c][0].wait_recv()
        first = send(x.at[c, 3, top], x.at[c, 2, top], fx_s.at[c, 2], fx_r.at[c, 2], at_x(1))
        fx[c][1].wait_recv()
        second = send(x.at[c, 1, bottom], x.at[c, 2, bottom], fx_s.at[c, 3], fx_r.at[c, 3], at_x(3))
        fw[c] = [first, second]

    def expand(c, first, last):
        for copy in fw[c] if c < LATE else efy[c - LATE]:
            copy.wait_recv()
        if first:
            wg_in.wait()
            wu_in.wait()

        def body(g, carry):
            block = x[c, g]
            gv = dot(block, wg[:, c * cc : (c + 1) * cc], ((1,), (1,)))
            uv = dot(block, wu[:, c * cc : (c + 1) * cc], ((1,), (1,)))
            if not first:
                gv = gv + accg[g]
                uv = uv + accu[g]
            if last:
                act[g] = (gv * jax.nn.sigmoid(gv) * uv).astype(BF16)
            else:
                accg[g] = gv
                accu[g] = uv
            return carry

        lax.fori_loop(0, NX, body, 0)

    for c in range(LATE):
        spread_z(c)
    for i in range(LATE + 3):
        if i < LATE:
            select(i)
        for c in (2 * i + 1, 2 * i + 2):
            if c < LATE:
                relay_z(c)
        for b in range(EARLY):
            if i == EARLY_Z_AT[b]:
                early_z(b)
            if i == EARLY_RELAY_AT[b]:
                early_relay(b)
        if 0 <= i - 1 < LATE:
            spread_x(i - 1)
        if 0 <= i - 2 < LATE:
            forward_x(i - 2)
        for b in range(EARLY):
            if i == SELECT_AT[b]:
                early_select(b)
        if 0 <= i - 3 < LATE:
            expand(i - 3, i == 3, i == LATE + 2 and EXPAND_AT[-1] != i)
        for b in range(EARLY):
            if i == EXPAND_AT[b]:
                expand(LATE + b, False, i == LATE + 2 and b == EARLY - 1)
        if i == 2:
            path_in.wait()
            write_pages(kt, fresh_ref, path_ref[...], position - length, count_ref[0])
            page_out = pltpu.make_async_copy(kt, newp_hbm, w_sem.at[16])
            page_out.start()

    wd_in.wait()
    gx, gw, gy, gz = {}, {}, {}, {}
    egy, egz, egx = {}, {}, {}

    def contract(c):
        top, bottom = pl.ds(0, half), pl.ds(half, half)

        def body(j, carry):
            g = (3 + j) % NX
            p[c, g] = dot(act[g], wd[:, c * cc : (c + 1) * cc]).astype(BF16)
            return carry

        if c < LATE:
            body(3, 0)
            gx[c] = [
                send(p.at[c, 2, top], a1.at[c], gx_s.at[c, 0], gx_r.at[c, 0], at_x(1)),
                send(p.at[c, 2, bottom], a3.at[c], gx_s.at[c, 1], gx_r.at[c, 1], at_x(3)),
            ]
            lax.fori_loop(0, 3, body, 0)
        else:
            b = c - LATE
            lax.fori_loop(0, 4, body, 0)
            egy[b] = [
                send(
                    p.at[c, :, pl.ds(d * slots, slots)], ev.at[b, flip_y(d)],
                    egy_s.at[b, d], egy_r.at[b, flip_y(d)], at_y(d),
                )
                for d in (1, 2, 6, 3, 7, 4, 5)
            ]
            ev[b, 0] = p[c, :, 0:slots]

    def back_start(src, dst, ss, rs):
        low, high = pl.ds(0, tree // 2), pl.ds(tree // 2, tree // 2)
        if len(src.shape) == 3:
            parts = [src.at[4, low], dst.at[4, low], src.at[4, high], dst.at[4, high]]
        else:
            parts = [src.at[4, :, low], dst.at[4, :, low], src.at[4, :, high], dst.at[4, :, high]]
        return [
            send(src.at[3], dst.at[3], ss.at[3], rs.at[3], at_z(1)),
            send(src.at[5], dst.at[5], ss.at[5], rs.at[5], at_z(7)),
            send(parts[0], parts[1], ss.at[4], rs.at[4], at_z(2)),
            send(parts[2], parts[3], ss.at[0], rs.at[0], at_z(6)),
            send(src.at[1], dst.at[7], ss.at[1], rs.at[7], at_z(1)),
            send(src.at[7], dst.at[1], ss.at[7], rs.at[1], at_z(7)),
        ]

    def back_relay(src, dst, ss, rs, copies):
        for copy in copies[:4]:
            copy.wait_recv()
        cut = tree // 2
        src[2] = (src[2].astype(F32) + dst[3].astype(F32)).astype(BF16)
        src[6] = (src[6].astype(F32) + dst[5].astype(F32)).astype(BF16)
        if len(src.shape) == 3:
            src[2, 0:cut] = (src[2, 0:cut].astype(F32) + dst[4, 0:cut].astype(F32)).astype(BF16)
            src[6, cut:] = (src[6, cut:].astype(F32) + dst[4, cut:].astype(F32)).astype(BF16)
        else:
            src[2, :, 0:cut] = (src[2, :, 0:cut].astype(F32) + dst[4, :, 0:cut].astype(F32)).astype(BF16)
            src[6, :, cut:] = (src[6, :, cut:].astype(F32) + dst[4, :, cut:].astype(F32)).astype(BF16)
        return copies[4:] + [
            send(src.at[2], dst.at[6], ss.at[2], rs.at[6], at_z(2)),
            send(src.at[6], dst.at[2], ss.at[6], rs.at[2], at_z(6)),
        ]

    def early_back_z(b):
        for copy in egy[b]:
            copy.wait_recv()

        def body(g, carry):
            part = dot(wt[g], ev[b, :, g].reshape(rows, cc))
            ezsend[b, :, g] = part.astype(BF16).reshape(NZ, tree, cc)
            return carry

        lax.fori_loop(0, NX, body, 0)
        egz[b] = back_start(ezsend.at[b], ezrecv.at[b], egz_s.at[b], egz_r.at[b])

    def early_back_relay(b):
        egz[b] = back_relay(ezsend.at[b], ezrecv.at[b], egz_s.at[b], egz_r.at[b], egz[b])

    def early_back_x(b):
        for copy in egz[b]:
            copy.wait_recv()
        total = ezsend[b, 0].astype(F32)
        for k in near:
            total = total + ezrecv[b, k].astype(F32)
        exsend[b] = total.astype(BF16)
        egx[b] = [
            send(exsend.at[b, k], exrecv.at[b, NX - k], egx_s.at[b, k], egx_r.at[b, NX - k], at_x(k))
            for k in (1, 3, 2)
        ]

    def early_finish(b):
        for copy in egx[b]:
            copy.wait_recv()
        c = LATE + b
        total = mixed[c].astype(F32) + exsend[b, 0].astype(F32)
        for k in range(1, NX):
            total = total + exrecv[b, k].astype(F32)
        out_ref[:, c * cc : (c + 1) * cc] = total.astype(BF16)

    def gather_x(c):
        gx[c][0].wait_recv()
        p[c, 1, 0:half] = (p[c, 1, 0:half].astype(F32) + a1[c].astype(F32)).astype(BF16)
        first = send(p.at[c, 1], bl.at[c], gx_s.at[c, 2], gx_r.at[c, 2], at_x(1))
        gx[c][1].wait_recv()
        p[c, 3, half:rows] = (p[c, 3, half:rows].astype(F32) + a3[c].astype(F32)).astype(BF16)
        second = send(p.at[c, 3], br.at[c], gx_s.at[c, 3], gx_r.at[c, 3], at_x(3))
        gw[c] = [first, second]

    def back_y(c):
        for copy in gw[c]:
            copy.wait_recv()
        total = p[c, 0].astype(F32) + bl[c].astype(F32) + br[c].astype(F32)
        total = total.astype(BF16).reshape(2 * NY, slots, cc)
        v[c, 0] = total[0]
        zz[c] = total
        gy[c] = [
            send(zz.at[c, d], v.at[c, flip_y(d)], gy_s.at[c, d], gy_r.at[c, flip_y(d)], at_y(d))
            for d in (1, 2, 6, 3, 7, 4, 5)
        ]

    def back_z(c):
        for copy in gy[c]:
            copy.wait_recv()
        part = dot(wt[0], v[c].reshape(rows, cc))
        zsend[c] = part.astype(BF16).reshape(NZ, tree, cc)
        if c < LATE - 1:
            gz[c] = back_start(zsend.at[c], zrecv.at[c], gz_s.at[c], gz_r.at[c])
        else:
            gz[c] = [
                send(zsend.at[c, k], zrecv.at[c, NZ - k], gz_s.at[c, k], gz_r.at[c, NZ - k], at_z(k)) for k in far
            ]

    def relay_back(c):
        if c < LATE - 1:
            gz[c] = back_relay(zsend.at[c], zrecv.at[c], gz_s.at[c], gz_r.at[c], gz[c])

    def finish(c):
        for copy in gz[c]:
            copy.wait_recv()
        total = mixed[c].astype(F32) + zsend[c, 0].astype(F32)
        for k in near if c < LATE - 1 else far:
            total = total + zrecv[c, k].astype(F32)
        out_ref[:, c * cc : (c + 1) * cc] = total.astype(BF16)

    for i in range(LATE + 4):
        if i < LATE:
            contract(i)
        if 0 <= i - 1 < LATE:
            gather_x(i - 1)
        for b in range(EARLY):
            if i == CONTRACT_AT[b]:
                contract(LATE + b)
        if 0 <= i - 2 < LATE:
            back_y(i - 2)
        if 0 <= i - 3 < LATE:
            back_z(i - 3)
        if 0 <= i - 4 < LATE:
            relay_back(i - 4)
        for b in range(EARLY):
            if i == BACK_Z_AT[b]:
                early_back_z(b)
            if i == BACK_RELAY_AT[b]:
                early_back_relay(b)
            if i == BACK_X_AT[b]:
                early_back_x(b)
        if 0 <= i - 5 < LATE:
            finish(i - 5)
    finish(LATE - 1)
    for b in range(EARLY):
        early_finish(b)

    for copy in started:
        copy.wait_send()
    page_out.wait()


def constants(cap):
    slots = 2 * NY * cap
    i = np.arange(NZ * slots)
    table = np.zeros((NZ * slots, 128), np.int32)
    for n, column in enumerate((i // slots, (i % slots) // cap, i % cap)):
        table[:, n] = column
    return table


def run_layer(
    hidden, queries, fresh, pages_t, page_table, cache_len, parents, accept_path, accept_count,
    key_up, value_up, out_proj, gain, ids, weights, wg_t, wu_t, w_down,
):
    tree, width = hidden.shape
    cc = width // CHUNKS
    hid = w_down.shape[0]
    n_heads = key_up.shape[0]
    cap = max(2, min(tree, 2 * tree * ids.shape[1] // (NZ * NY * 2)))
    slots = 2 * NY * cap
    rows = NZ * slots
    cols = NZ * tree
    smem = pl.BlockSpec(memory_space=pltpu.SMEM)
    vmem = pl.BlockSpec(memory_space=pltpu.VMEM)
    hbm = pl.BlockSpec(memory_space=pl.ANY)
    dma = pltpu.SemaphoreType.DMA
    c = CHUNKS
    staged = [
        hidden, queries, fresh, parents, accept_path, gain, ids, weights, jnp.asarray(constants(cap)),
        pages_t, key_up, value_up, out_proj, wg_t, wu_t, w_down,
    ]
    return pl.pallas_call(
        layer_kernel,
        out_shape=(jax.ShapeDtypeStruct((tree, width), BF16), jax.ShapeDtypeStruct(pages_t.shape, BF16)),
        in_specs=[smem] * 3 + [hbm] * 16,
        out_specs=(vmem, hbm),
        scratch_shapes=[pltpu.VMEM(value.shape, value.dtype) for value in staged]
        + [
            pltpu.VMEM(shape, dtype)
            for shape, dtype in (
                ((n_heads * tree, fresh.shape[1]), BF16),
                ((n_heads * tree, key_up.shape[2]), BF16),
                ((NX, tree, width), BF16),
                ((NX, tree, width // NX), BF16),
                ((NX, tree, width // NX), BF16),
                ((c, tree, cc), BF16),
                ((NZ, NX, 16, 128), BF16),
                ((NX, rows, cols), BF16),
                ((NX, cols, rows), BF16),
                ((LATE, NZ, tree, cc), BF16),
                ((LATE, 2 * NY, slots, cc), BF16),
                ((c, NX, rows, cc), BF16),
                ((NX, rows, hid), F32),
                ((NX, rows, hid), F32),
                ((NX, rows, hid), BF16),
                ((c, NX, rows, cc), BF16),
                ((LATE, rows // 2, cc), BF16),
                ((LATE, rows // 2, cc), BF16),
                ((LATE, rows, cc), BF16),
                ((LATE, rows, cc), BF16),
                ((LATE, 2 * NY, slots, cc), BF16),
                ((LATE, 2 * NY, slots, cc), BF16),
                ((LATE, NZ, tree, cc), BF16),
                ((LATE, NZ, tree, cc), BF16),
                ((EARLY, NZ, NX, tree, cc), BF16),
                ((EARLY, 2 * NY, NX, slots, cc), BF16),
                ((EARLY, 2 * NY, NX, slots, cc), BF16),
                ((EARLY, NZ, NX, tree, cc), BF16),
                ((EARLY, NZ, NX, tree, cc), BF16),
                ((EARLY, NX, tree, cc), BF16),
                ((EARLY, NX, tree, cc), BF16),
            )
        ]
        + [
            dma(shape)
            for shape in [(17,)]
            + [(NX,)] * 6
            + [(NZ,)] * 2
            + [(LATE, NZ)] * 2
            + [(LATE, 2 * NY)] * 2
            + [(LATE, 4)] * 4
            + [(LATE, 2 * NY)] * 2
            + [(LATE, NZ)] * 2
            + [(EARLY, NX)] * 2
            + [(EARLY, NZ)] * 2
            + [(EARLY, 2 * NY)] * 4
            + [(EARLY, NZ)] * 2
            + [(EARLY, NX)] * 2
        ],
        compiler_params=pltpu.CompilerParams(
            collective_id=0, has_side_effects=True, vmem_limit_bytes=60 * 1024 * 1024
        ),
        name="layer",
    )(page_table, cache_len, accept_count, *staged)


def local(
    hidden, queries, new_latent, pages, page_table, cache_len, parents, accept_path, accept_count,
    key_up, value_up, out_proj, norm_gain, route_ids, route_weights, w_gate, w_up, w_down,
):
    layer_out, pages_out = run_layer(
        hidden[0], queries[0], new_latent[0], jnp.swapaxes(pages, 1, 2), page_table, cache_len, parents,
        accept_path, accept_count, key_up, value_up, out_proj, norm_gain.reshape(-1, 128),
        jnp.transpose(route_ids, (0, 3, 1, 2)), jnp.transpose(route_weights, (0, 3, 1, 2)),
        jnp.swapaxes(w_gate[0], 0, 1), jnp.swapaxes(w_up[0], 0, 1), w_down[0],
    )
    return (layer_out[None], jnp.swapaxes(pages_out, 1, 2))


def solution(mesh):
    in_specs = (
        P(("req", "exp"), None, None),
        P(("req", "exp"), None, None),
        P(("req", "exp"), None, None),
        P(("req", "exp"), None, None),
        P(("req", "exp"), None),
        P(("req", "exp")),
        P(("req", "exp"), None),
        P(("req", "exp"), None),
        P(("req", "exp")),
        P(),
        P(),
        P(None, "req"),
        P(),
        P(None, "exp", None, None),
        P(None, "exp", None, None),
        P("exp", None, "req"),
        P("exp", None, "req"),
        P("exp", "req", None),
    )
    out_specs = (P(("req", "exp"), None, None), P(("req", "exp"), None, None))
    return jax.shard_map(local, mesh=mesh, in_specs=in_specs, out_specs=out_specs, check_vma=False)
```
